32 devices in a mesh: path: 4 (over z), trade: 8 (over y, x, core).
Axes of the slice: x: 2, y: 2, z: 4, core: 2. Of those that a mesh axis runs over, the one named last changes fastest.
Arguments:
- factors: bfloat16 [32, 8, 512], P(None, None, 'path'), may hold values from -5 to 5
- loadings: bfloat16 [32, 8, 32768], P(None, None, 'trade'), may hold values from -0.5 to 0.5
- notional: float32 [32768], P('trade'), may hold values from -1 to 1
- strike: float32 [32768], P('trade'), may hold values from 0.5 to 1.5
- date_weight: float32 [32], replicated, may hold values from 0.3 to 3
- loss_spanning: float32 [128], replicated, may hold values from 0.2 to 0.9
- loss_local: float32 [1024], P('trade'), may hold values from 0.2 to 0.9
- trade_slot: int32 [32768], P('trade'), may hold values from 0 to 255
- span_list: int32 [1024], P('trade'), may hold values from 0 to 127, as said below
Outputs:
- loading_grad: float32 [32, 8, 32768], P('path', None, 'trade')
- factor_grad: float32 [32, 8, 512], P('trade', None, 'path')
The draws below stay inside these ranges and needn't reach their ends.
Inputs may be any that keep to these rules, and one draw needn't show every extreme that they name: `trade_slot`: slot s < 128 of a trade shard holds that shard's spanning set from span_list; slot 128 + i holds the shard's i-th local set. `span_list`: the 128 entries of one trade shard are distinct spanning set ids.
All inputs are finite; a program needn't handle non-finite values.
Results may differ from the reference program's by a relative error of at most 0.0021.
Values may be sent and summed in bfloat16 or wider, within the bound.
A program may use at most 64 MiB of HBM per device.

```python
import math
import jax
import jax.numpy as jnp
import numpy as np
from jax import lax

FACTORS = 8
DATES = 32
K_DEV = 4096
SLOTS = 256
SPAN_DEV = 128
LOC_DEV = 128
SPAN_ALL = 128
TRADES = 32768
PATHS = 512
N_TRADE = 8


def draw_span_list(key, part):
    shard_keys = jax.random.split(jax.random.fold_in(key, 11), N_TRADE)
    shards = jnp.arange(N_TRADE, dtype=jnp.int32)

    def one_shard(shard_key, shard):
        order = jax.random.permutation(shard_key, SPAN_ALL).astype(jnp.int32)
        wanted = (shard * (SPAN_ALL - 1) // max(N_TRADE - 1, 1)).astype(jnp.int32)
        position = jnp.argmax(order == wanted)
        leading = order[0]
        order = order.at[position].set(leading).at[0].set(wanted)
        return order[:SPAN_DEV]
    return jax.vmap(one_shard)(shard_keys, shards).reshape(N_TRADE * SPAN_DEV)


def with_ends(result, rng, least, high):
    extent = result.shape
    spot = [jax.random.randint(jax.random.fold_in(rng, axis), (), 0, extent[axis]) for axis in range(len(extent))]
    result = result.at[tuple(spot)].set(least)
    longest = extent.index(max(extent))
    spot[longest] = (spot[longest] + 1) % extent[longest]
    return result.at[tuple(spot)].set(high)


def steps_of(key, extent, cuts, smallest, largest):
    level, own = 1.0, jax.random.fold_in(key, 6)
    for dim, blocks in cuts:
        draws = jnp.exp(jax.random.uniform(jax.random.fold_in(own, dim), (blocks,), jnp.float32, smallest / len(cuts), largest / len(cuts)))
        level = level * jnp.repeat(draws, extent[dim] // blocks).reshape([-1 if axis == dim else 1 for axis in range(len(extent))])
    return level


def rank_table(count, skew):
    portions = [(1 << 20) // math.isqrt(rank ** skew) + 1 for rank in range(1, count + 1)]
    deviation = 1 + sum(portions) // (1 << 30)
    return np.cumsum(np.array([max(1, weight // deviation) for weight in portions]))


def ranked(key, dims, amount, skew):
    grid = rank_table(amount, skew)
    ticket = jax.random.randint(jax.random.fold_in(key, 1), dims, 0, int(grid[amount - 1]))
    grade = jnp.searchsorted(jnp.asarray(grid, jnp.int32), ticket, side="right")
    return jax.random.permutation(jax.random.fold_in(key, 2), amount)[grade].astype(jnp.int32)


def normal_values(key, dims, spread, limit, cuts=(), held_as=jnp.bfloat16):
    gain = steps_of(key, dims, cuts, -0.22, 0.18) if cuts else 1.0
    drawn = jax.random.normal(key, dims, jnp.float32) * spread * gain
    return jnp.minimum(jnp.maximum(drawn, -limit), limit).astype(held_as)


def setup_inputs(seed: int = 0) -> dict:
    key_list = jax.random.split(jax.random.key(seed), 10)
    return {
        "factors": normal_values(key_list[0], (DATES, FACTORS, PATHS), 1.0, 5.0, ((2, 4),)),
        "loadings": normal_values(key_list[1], (DATES, FACTORS, TRADES), 0.12, 0.5, ((2, 8),)),
        "notional": jnp.clip(jax.random.uniform(key_list[2], (TRADES,), jnp.float32, -1.0, 1.0) * steps_of(key_list[2], (TRADES,), ((0, 8),), -0.4, 0.0), -1.0, 1.0),
        "strike": jnp.clip(0.5 + 1.0 * jax.random.uniform(key_list[3], (TRADES,), jnp.float32) ** steps_of(key_list[3], (TRADES,), ((0, 8),), -0.2, 0.2), 0.5, 1.5),
        "date_weight": jnp.clip(jnp.exp(jax.random.uniform(key_list[4], (DATES,), jnp.float32, math.log(0.3), math.log(3.0))), 0.3, 3.0),
        "loss_spanning": jnp.clip(jax.random.uniform(key_list[5], (SPAN_ALL,), jnp.float32, 0.2, 0.9), 0.2, 0.9),
        "loss_local": jnp.clip(0.2 + 0.7 * jax.random.uniform(key_list[6], (N_TRADE * LOC_DEV,), jnp.float32) ** steps_of(key_list[6], (N_TRADE * LOC_DEV,), ((0, 8),), -0.2, 0.2), 0.2, 0.9),
        "trade_slot": with_ends(ranked(key_list[7], (TRADES,), SLOTS, 2), jax.random.fold_in(key_list[7], 3), 0, SLOTS - 1).astype(jnp.int32),
        "span_list": draw_span_list(jax.random.fold_in(key_list[9], 71), 0),
    }


smoothing = 0.5


def reference(factors, loadings, notional, strike, date_weight, loss_spanning, loss_local, trade_slot, span_list):
    shard_of = (jnp.arange(TRADES) // K_DEV).astype(jnp.int32)
    global_slot = (shard_of * SLOTS + trade_slot).astype(jnp.int32)
    path_count = factors.shape[2]

    def one_date(date_index):
        factor_now = factors[date_index]
        loading_now = loadings[date_index]
        exponent = jnp.dot(factor_now.T, loading_now, preferred_element_type=jnp.float32)
        growth = jnp.exp(exponent)
        values = (notional[None, :] * (growth - strike[None, :])).astype(jnp.bfloat16)
        partial_sums = jax.ops.segment_sum(values.astype(jnp.float32).T, global_slot, N_TRADE * SLOTS).T
        partial_sums = partial_sums.reshape(path_count, N_TRADE, SLOTS)
        span_part = partial_sums[:, :, :SPAN_DEV].reshape(path_count, N_TRADE * SPAN_DEV)
        span_total = jax.ops.segment_sum(span_part.T, span_list, SPAN_ALL).T
        weight_now = date_weight[date_index]
        span_weight = (weight_now * loss_spanning[None, :] * jax.nn.sigmoid(span_total / smoothing)).astype(jnp.bfloat16)
        local_total = partial_sums[:, :, SPAN_DEV:].reshape(path_count, N_TRADE * LOC_DEV)
        local_weight = (weight_now * loss_local[None, :] * jax.nn.sigmoid(local_total / smoothing)).astype(jnp.bfloat16)
        span_slots = span_weight[:, span_list].reshape(path_count, N_TRADE, SPAN_DEV)
        slot_weight = jnp.concatenate([span_slots, local_weight.reshape(path_count, N_TRADE, LOC_DEV)], axis=2)
        slot_weight = slot_weight.reshape(path_count, N_TRADE * SLOTS)
        trade_weight = slot_weight[:, global_slot].astype(jnp.float32)
        sensitivity = (trade_weight * notional[None, :] * growth).astype(jnp.bfloat16)
        loading_grad = jnp.dot(factor_now, sensitivity, preferred_element_type=jnp.float32) / path_count
        factor_grad = jnp.dot(loading_now, sensitivity.T, preferred_element_type=jnp.float32)
        return loading_grad, factor_grad

    loading_grads, factor_grads = lax.map(one_date, jnp.arange(DATES).astype(jnp.int32))
    return loading_grads, factor_grads
```

```python
import functools
import math

import jax
import jax.numpy as jnp
from jax import lax
from jax.experimental import pallas as pl
from jax.experimental.pallas import tpu as pltpu
from jax.sharding import PartitionSpec as P

smoothing = 0.5
MESH = pl.DeviceIdType.MESH
chunk = 512
bf16 = jnp.bfloat16
f32 = jnp.float32


def dot(a, b):
    return jnp.dot(a, b, preferred_element_type=f32)


def kernel(
    n_path,
    n_trade,
    factors_ref,
    loadings_ref,
    notional_ref,
    strike_ref,
    date_weight_ref,
    loss_span_ref,
    loss_local_ref,
    slot_ref,
    span_ref,
    loading_grad_ref,
    factor_grad_ref,
    growth,
    table,
    table_t,
    load_own,
    load_wide,
    load_t,
    offset,
    fac_recv,
    fac,
    fac_t,
    total,
    part,
    part_recv,
    local_w,
    span_w,
    span_recv,
    slot_w,
    factor_acc,
    factor_t,
    grad_send,
    grad_recv,
    load_sem,
    fac_ssem,
    fac_rsem,
    part_ssem,
    part_rsem,
    span_ssem,
    span_rsem,
    grad_ssem,
    grad_rsem,
):
    me_path = lax.axis_index("path")
    me_trade = lax.axis_index("trade")
    dates, factor_count, path_local = factors_ref.shape
    dates_own = dates // n_path
    dates_out = dates // n_trade
    groups = dates_own // dates_out
    trades = loadings_ref.shape[2]
    spans = loss_span_ref.shape[1]
    span_slots = span_ref.shape[1]
    locals_ = loss_local_ref.shape[1]
    slots = span_slots + locals_
    path_total = n_path * path_local
    steps = trades // chunk
    first_date = me_path * dates_own

    def path_at(step):
        return lax.rem(me_path + step + n_path, n_path)

    def trade_at(step):
        return lax.rem(me_trade + step + n_trade, n_trade)

    def columns(c):
        return pl.ds(pl.multiple_of(c * chunk, chunk), chunk)

    load = pltpu.make_async_copy(
        loadings_ref.at[pl.ds(first_date, dates_own)], load_own, load_sem
    )
    load.start()

    barrier = pltpu.get_barrier_semaphore()
    for a in range(n_path):
        for b in range(n_trade):
            if a or b:
                pl.semaphore_signal(
                    barrier,
                    inc=1,
                    device_id={"path": path_at(a), "trade": trade_at(b)},
                    device_id_type=MESH,
                )
    pl.semaphore_wait(barrier, n_path * n_trade - 1)

    def fac_copy(o):
        there = path_at(o)
        return pltpu.make_async_remote_copy(
            src_ref=factors_ref.at[pl.ds(there * dates_own, dates_own)],
            dst_ref=fac_recv.at[o - 1],
            send_sem=fac_ssem,
            recv_sem=fac_rsem,
            device_id={"path": there},
            device_id_type=MESH,
        )

    for o in range(1, n_path):
        fac_copy(o).start()

    set_match = (
        lax.broadcasted_iota(jnp.int32, (spans, span_slots), 0) == span_ref[...]
    ).astype(f32).astype(bf16)

    @pl.loop(0, steps)
    def _(c):
        cols = columns(c)
        hot = (
            lax.broadcasted_iota(jnp.int32, (slots, chunk), 0) == slot_ref[:, cols]
        ).astype(f32)
        span_hot = dot(set_match, hot[:span_slots].astype(bf16))
        both = jnp.concatenate([span_hot, hot[span_slots:]], axis=0)
        table_t[:, cols] = both.astype(bf16)
        table[cols, :] = both.T.astype(bf16)

    offset[...] = notional_ref[...] * strike_ref[...]
    load.wait()

    for d in range(dates_own):
        row = load_own[d]
        load_wide[d] = jnp.concatenate([row, row, row, row], axis=0)

    @pl.loop(0, steps)
    def _(c):
        cols = columns(c)
        rows = [load_own[d, :, cols].astype(f32) for d in range(dates_own)]
        load_t[cols, :] = jnp.concatenate(rows, axis=0).T.astype(bf16)

    if n_path > 1:
        pltpu.make_async_copy(fac_recv, fac_recv, fac_rsem).wait()

    for d in range(dates_own):
        blocks = [factors_ref[first_date + d]]
        blocks += [fac_recv[o - 1, d] for o in range(1, n_path)]
        whole = jnp.concatenate(blocks, axis=1)
        fac[d] = whole
        scaled = whole.astype(f32) * f32(math.log2(math.e))
        high = scaled.astype(bf16).astype(f32)
        middle = (scaled - high).astype(bf16).astype(f32)
        low = scaled - high - middle
        split = jnp.concatenate([high, middle, low, jnp.zeros_like(low)], axis=0)
        fac_t[d] = split.T.astype(bf16)

    def part_copy(d, o):
        there = trade_at(o)
        return pltpu.make_async_remote_copy(
            src_ref=part.at[d, there],
            dst_ref=part_recv.at[d, o - 1],
            send_sem=part_ssem.at[d],
            recv_sem=part_rsem.at[d],
            device_id={"trade": there},
            device_id_type=MESH,
        )

    def span_copy(d, o):
        return pltpu.make_async_remote_copy(
            src_ref=span_w.at[d],
            dst_ref=span_recv.at[d, o - 1],
            send_sem=span_ssem.at[d],
            recv_sem=span_rsem.at[d],
            device_id={"trade": trade_at(o)},
            device_id_type=MESH,
        )

    def wait_all(buffer, sem):
        pltpu.make_async_copy(buffer, buffer, sem).wait()

    def finish_span(d):
        wait_all(part_recv.at[d], part_rsem.at[d])
        sums = part[d, me_trade]
        for o in range(1, n_trade):
            sums = sums + part_recv[d, o - 1]
        weight = date_weight_ref[first_date + d]
        span_w[d] = (
            weight * loss_span_ref[...] * jax.nn.sigmoid(sums / smoothing)
        ).astype(bf16)
        for o in range(1, n_trade):
            span_copy(d, o).start()

    @pl.loop(0, dates_own)
    def _(d):
        total[...] = jnp.zeros_like(total)

        @pl.loop(0, steps)
        def _(c):
            cols = columns(c)
            exponent = dot(fac_t[d], load_wide[d, :, cols])
            grown = jnp.exp2(exponent) * notional_ref[:, cols]
            growth[d * steps + c] = grown.astype(bf16)
            values = (grown - offset[:, cols]).astype(bf16)
            total[...] += dot(values, table[cols, :])

        part[d] = total[:, :spans].reshape(part.shape[1:])
        for o in range(1, n_trade):
            part_copy(d, o).start()
        weight = date_weight_ref[first_date + d]
        local_w[d] = (
            weight * loss_local_ref[...] * jax.nn.sigmoid(total[:, spans:] / smoothing)
        ).astype(bf16)

        @pl.when(d > 0)
        def _():
            finish_span(d - 1)

    if dates_own == 1:
        finish_span(0)

    def grad_copy(g, o):
        return pltpu.make_async_remote_copy(
            src_ref=grad_send.at[g, o],
            dst_ref=grad_recv.at[me_trade],
            send_sem=grad_ssem.at[g, o],
            recv_sem=grad_rsem.at[me_trade],
            device_id={"path": path_at(-o), "trade": me_path * groups + g},
            device_id_type=MESH,
        )

    rows = path_total // n_trade

    @pl.loop(0, dates_own)
    def _(d):
        wait_all(span_recv.at[d], span_rsem.at[d])
        slot_w[pl.ds(pl.multiple_of(me_trade * rows, rows), rows), :spans] = span_w[d]
        for o in range(1, n_trade):
            start = pl.multiple_of(trade_at(-o) * rows, rows)
            slot_w[pl.ds(start, rows), :spans] = span_recv[d, o - 1]
        slot_w[:, spans:] = local_w[d]
        factor_acc[...] = jnp.zeros_like(factor_acc)

        @pl.loop(0, steps)
        def _(c):
            cols = columns(c)
            weight = dot(slot_w[...], table_t[:, cols]).astype(bf16)
            sensitivity = weight * growth[d * steps + c]
            loading_grad_ref[d, :, cols] = dot(fac[d], sensitivity) / path_total
            factor_acc[...] += dot(sensitivity, load_t[cols, :])

        factor_t[...] = factor_acc[...].T
        mine = factor_t[pl.ds(pl.multiple_of(d * factor_count, factor_count), factor_count), :]
        g = d // dates_out
        for o in range(n_path):
            grad_send[g, o, lax.rem(d, dates_out)] = mine[
                :, o * path_local : (o + 1) * path_local
            ]

        if dates_own > 1:

            @pl.when(d == 0)
            def _():
                finish_span(dates_own - 1)

        @pl.when(lax.rem(d, dates_out) == dates_out - 1)
        def _():
            here = me_path * groups + g == me_trade

            @pl.when(here)
            def _():
                pltpu.make_async_copy(
                    grad_send.at[g, 0], grad_recv.at[me_trade], grad_rsem.at[me_trade]
                ).start()

            @pl.when(jnp.logical_not(here))
            def _():
                grad_copy(g, 0).start()

            for o in range(1, n_path):
                grad_copy(g, o).start()

    if n_path > 1:
        wait_all(fac_recv, fac_ssem)
    for d in range(dates_own):
        wait_all(part_recv.at[d], part_ssem.at[d])
        wait_all(span_recv.at[d], span_ssem.at[d])
    for g in range(groups):

        @pl.when(me_path * groups + g != me_trade)
        def _():
            grad_copy(g, 0).wait_send()

        for o in range(1, n_path):
            grad_copy(g, o).wait_send()

    for b in range(n_trade):
        wait_all(grad_recv.at[b], grad_rsem.at[b])
    sums = grad_recv[0]
    for b in range(1, n_trade):
        sums = sums + grad_recv[b]
    factor_grad_ref[...] = sums


def on_device(
    n_path,
    n_trade,
    factors,
    loadings,
    notional,
    strike,
    date_weight,
    loss_spanning,
    loss_local,
    trade_slot,
    span_list,
):
    dates, factor_count, path_local = factors.shape
    trades = loadings.shape[2]
    spans = loss_spanning.shape[0]
    locals_ = loss_local.shape[0]
    width = spans + locals_
    paths = n_path * path_local
    rows = paths // n_trade
    dates_own = dates // n_path
    dates_out = dates // n_trade
    groups = dates_own // dates_out
    vmem = pl.BlockSpec(memory_space=pltpu.VMEM)
    dma = pltpu.SemaphoreType.DMA
    return pl.pallas_call(
        functools.partial(kernel, n_path, n_trade),
        out_shape=(
            jax.ShapeDtypeStruct((dates_own, factor_count, trades), f32),
            jax.ShapeDtypeStruct((dates_out, factor_count, path_local), f32),
        ),
        in_specs=[
            vmem,
            pl.BlockSpec(memory_space=pl.ANY),
            vmem,
            vmem,
            pl.BlockSpec(memory_space=pltpu.SMEM),
            vmem,
            vmem,
            vmem,
            vmem,
        ],
        out_specs=(vmem, vmem),
        scratch_shapes=[
            pltpu.VMEM((dates_own * (trades // chunk), paths, chunk), bf16),
            pltpu.VMEM((trades, width), bf16),
            pltpu.VMEM((width, trades), bf16),
            pltpu.VMEM((dates_own, factor_count, trades), bf16),
            pltpu.VMEM((dates_own, 4 * factor_count, trades), bf16),
            pltpu.VMEM((trades, dates_own * factor_count), bf16),
            pltpu.VMEM((1, trades), f32),
            pltpu.VMEM((max(n_path - 1, 1), dates_own, factor_count, path_local), bf16),
            pltpu.VMEM((dates_own, factor_count, paths), bf16),
            pltpu.VMEM((dates_own, paths, 4 * factor_count), bf16),
            pltpu.VMEM((paths, width), f32),
            pltpu.VMEM((dates_own, n_trade, rows, spans), f32),
            pltpu.VMEM((dates_own, n_trade - 1, rows, spans), f32),
            pltpu.VMEM((dates_own, paths, locals_), bf16),
            pltpu.VMEM((dates_own, rows, spans), bf16),
            pltpu.VMEM((dates_own, n_trade - 1, rows, spans), bf16),
            pltpu.VMEM((paths, width), bf16),
            pltpu.VMEM((paths, dates_own * factor_count), f32),
            pltpu.VMEM((dates_own * factor_count, paths), f32),
            pltpu.VMEM((groups, n_path, dates_out, factor_count, path_local), f32),
            pltpu.VMEM((n_trade, dates_out, factor_count, path_local), f32),
            dma,
            dma,
            dma,
            dma((dates_own,)),
            dma((dates_own,)),
            dma((dates_own,)),
            dma((dates_own,)),
            dma((groups, n_path)),
            dma((n_trade,)),
        ],
        compiler_params=pltpu.CompilerParams(
            collective_id=0, has_side_effects=True, vmem_limit_bytes=67043328
        ),
    )(
        factors,
        loadings,
        notional[None],
        strike[None],
        date_weight,
        loss_spanning[None],
        loss_local[None],
        trade_slot[None],
        span_list[None],
    )


def solution(mesh):
    return jax.shard_map(
        functools.partial(on_device, mesh.shape["path"], mesh.shape["trade"]),
        mesh=mesh,
        in_specs=(
            P(None, None, "path"),
            P(None, None, "trade"),
            P("trade"),
            P("trade"),
            P(),
            P(),
            P("trade"),
            P("trade"),
            P("trade"),
        ),
        out_specs=(P("path", None, "trade"), P("trade", None, "path")),
        check_vma=False,
    )
```

```python
import functools
import math

import jax
import jax.numpy as jnp
from jax import lax
from jax.experimental import pallas as pl
from jax.experimental.pallas import tpu as pltpu
from jax.sharding import PartitionSpec as P

smoothing = 0.5
MESH = pl.DeviceIdType.MESH
bf16 = jnp.bfloat16
f32 = jnp.float32


def chunk_of(paths, trades):
    return math.gcd(trades, (1 << 20) // paths)


def dot(a, b):
    return jnp.dot(a, b, preferred_element_type=f32)


def kernel(
    n_path,
    n_trade,
    factors_ref,
    loadings_ref,
    notional_ref,
    strike_ref,
    date_weight_ref,
    loss_span_ref,
    loss_local_ref,
    slot_ref,
    span_ref,
    loading_grad_ref,
    factor_grad_ref,
    growth,
    table,
    table_t,
    load_own,
    load_wide,
    load_t,
    offset,
    fac_recv,
    fac,
    fac_t,
    total,
    part,
    pair_recv,
    chip_sum,
    cross_recv,
    local_w,
    span_half,
    span_other,
    slot_w,
    factor_acc,
    factor_t,
    grad_send,
    grad_recv,
    load_sem,
    fac_ssem,
    fac_rsem,
    pair_ssem,
    pair_rsem,
    cross_ssem,
    cross_rsem,
    half_ssem,
    half_rsem,
    other_ssem,
    other_rsem,
    grad_ssem,
    grad_rsem,
):
    me_path = lax.axis_index("path")
    me_trade = lax.axis_index("trade")
    dates, factor_count, path_local = factors_ref.shape
    dates_own = dates // n_path
    dates_out = dates // n_trade
    groups = dates_own // dates_out
    trades = loadings_ref.shape[2]
    spans = loss_span_ref.shape[1]
    span_slots = span_ref.shape[1]
    locals_ = loss_local_ref.shape[1]
    slots = span_slots + locals_
    path_total = n_path * path_local
    chunk = chunk_of(path_total, trades)
    steps = trades // chunk
    first_date = me_path * dates_own
    rows = path_total // n_trade
    chips = n_trade // 2
    me_chip = me_trade // 2
    me_core = lax.rem(me_trade, 2)
    sibling = me_trade + 1 - 2 * me_core

    def path_at(step):
        return lax.rem(me_path + step + n_path, n_path)

    def trade_at(step):
        return lax.rem(me_trade + step + n_trade, n_trade)

    def chip_at(step):
        return lax.rem(me_chip + step + chips, chips)

    def columns(c):
        return pl.ds(pl.multiple_of(c * chunk, chunk), chunk)

    load = pltpu.make_async_copy(
        loadings_ref.at[pl.ds(first_date, dates_own)], load_own, load_sem
    )
    load.start()

    barrier = pltpu.get_barrier_semaphore()
    for a in range(n_path):
        for b in range(n_trade):
            if a or b:
                pl.semaphore_signal(
                    barrier,
                    inc=1,
                    device_id={"path": path_at(a), "trade": trade_at(b)},
                    device_id_type=MESH,
                )
    set_match = (
        lax.broadcasted_iota(jnp.int32, (spans, span_slots), 0) == span_ref[...]
    ).astype(f32).astype(bf16)

    @pl.loop(0, steps)
    def _(c):
        cols = columns(c)
        hot = (
            lax.broadcasted_iota(jnp.int32, (slots, chunk), 0) == slot_ref[:, cols]
        ).astype(f32)
        span_hot = dot(set_match, hot[:span_slots].astype(bf16))
        both = jnp.concatenate([span_hot, hot[span_slots:]], axis=0)
        table_t[:, cols] = both.astype(bf16)
        table[cols, :] = both.T.astype(bf16)

    pl.semaphore_wait(barrier, n_path * n_trade - 1)

    def fac_copy(o):
        there = path_at(o)
        return pltpu.make_async_remote_copy(
            src_ref=factors_ref.at[pl.ds(there * dates_own, dates_own)],
            dst_ref=fac_recv.at[o - 1],
            send_sem=fac_ssem,
            recv_sem=fac_rsem,
            device_id={"path": there},
            device_id_type=MESH,
        )

    for o in range(1, n_path):
        fac_copy(o).start()

    offset[...] = notional_ref[...] * strike_ref[...]
    load.wait()

    for d in range(dates_own):
        row = load_own[d]
        load_wide[d] = jnp.concatenate([row, row, row, row], axis=0)

    @pl.loop(0, steps)
    def _(c):
        cols = columns(c)
        rows = [load_own[d, :, cols].astype(f32) for d in range(dates_own)]
        load_t[cols, :] = jnp.concatenate(rows, axis=0).T.astype(bf16)

    if n_path > 1:
        pltpu.make_async_copy(fac_recv, fac_recv, fac_rsem).wait()

    for d in range(dates_own):
        blocks = [factors_ref[first_date + d]]
        blocks += [fac_recv[o - 1, d] for o in range(1, n_path)]
        whole = jnp.concatenate(blocks, axis=1)
        fac[d] = whole
        scaled = whole.astype(f32) * f32(math.log2(math.e))
        high = scaled.astype(bf16).astype(f32)
        middle = (scaled - high).astype(bf16).astype(f32)
        low = scaled - high - middle
        split = jnp.concatenate([high, middle, low, jnp.zeros_like(low)], axis=0)
        fac_t[d] = split.T.astype(bf16)

    def wait_all(buffer, sem):
        pltpu.make_async_copy(buffer, buffer, sem).wait()

    def send_pair(d):
        pltpu.make_async_remote_copy(
            src_ref=part.at[d, 1 - me_core],
            dst_ref=pair_recv.at[d],
            send_sem=pair_ssem.at[d],
            recv_sem=pair_rsem.at[d],
            device_id={"trade": sibling},
            device_id_type=MESH,
        ).start()

    def send_cross(d):
        wait_all(pair_recv.at[d], pair_rsem.at[d])
        chip_sum[d] = part[d, me_core] + pair_recv[d]
        for o in range(1, chips):
            there = chip_at(o)
            pltpu.make_async_remote_copy(
                src_ref=chip_sum.at[d, there],
                dst_ref=cross_recv.at[d, o - 1],
                send_sem=cross_ssem.at[d],
                recv_sem=cross_rsem.at[d],
                device_id={"trade": there * 2 + me_core},
                device_id_type=MESH,
            ).start()

    def send_half(d):
        wait_all(cross_recv.at[d], cross_rsem.at[d])
        sums = chip_sum[d, me_chip]
        for o in range(1, chips):
            sums = sums + cross_recv[d, o - 1]
        weight = date_weight_ref[first_date + d]
        span_half[d, 0] = (
            weight * loss_span_ref[...] * jax.nn.sigmoid(sums / smoothing)
        ).astype(bf16)
        for o in range(1, chips):
            pltpu.make_async_remote_copy(
                src_ref=span_half.at[d, 0],
                dst_ref=span_half.at[d, o],
                send_sem=half_ssem.at[d],
                recv_sem=half_rsem.at[d],
                device_id={"trade": chip_at(o) * 2 + me_core},
                device_id_type=MESH,
            ).start()

    def send_other(d):
        wait_all(span_half.at[d, pl.ds(1, chips - 1)], half_rsem.at[d])
        pltpu.make_async_remote_copy(
            src_ref=span_half.at[d],
            dst_ref=span_other.at[d],
            send_sem=other_ssem.at[d],
            recv_sem=other_rsem.at[d],
            device_id={"trade": sibling},
            device_id_type=MESH,
        ).start()

    stages = (send_cross, send_half, send_other)

    @pl.loop(0, dates_own)
    def _(d):
        total[...] = jnp.zeros_like(total)

        @pl.loop(0, steps)
        def _(c):
            cols = columns(c)
            exponent = dot(fac_t[d], load_wide[d, :, cols])
            grown = jnp.exp2(exponent) * notional_ref[:, cols]
            growth[d * steps + c] = grown.astype(bf16)
            values = (grown - offset[:, cols]).astype(bf16)
            total[...] += dot(values, table[cols, :])

        for r in range(n_trade):
            part[d, r % 2, r // 2] = total[r * rows : (r + 1) * rows, :spans]
        send_pair(d)
        weight = date_weight_ref[first_date + d]
        local_w[d] = (
            weight * loss_local_ref[...] * jax.nn.sigmoid(total[:, spans:] / smoothing)
        ).astype(bf16)

        for late, stage in enumerate(stages, 1):

            @pl.when(d >= late)
            def _(late=late, stage=stage):
                stage(d - late)

    def grad_copy(g, o):
        return pltpu.make_async_remote_copy(
            src_ref=grad_send.at[g, o],
            dst_ref=grad_recv.at[me_trade],
            send_sem=grad_ssem.at[g, o],
            recv_sem=grad_rsem.at[me_trade],
            device_id={"path": path_at(-o), "trade": me_path * groups + g},
            device_id_type=MESH,
        )

    @pl.loop(0, dates_own)
    def _(d):
        wait_all(span_other.at[d], other_rsem.at[d])
        for o in range(chips):
            for core, source in ((me_core, span_half), (1 - me_core, span_other)):
                start = pl.multiple_of((chip_at(-o) * 2 + core) * rows, rows)
                slot_w[pl.ds(start, rows), :spans] = source[d, o]
        slot_w[:, spans:] = local_w[d]
        factor_acc[...] = jnp.zeros_like(factor_acc)

        @pl.loop(0, steps)
        def _(c):
            cols = columns(c)
            weight = dot(slot_w[...], table_t[:, cols]).astype(bf16)
            sensitivity = weight * growth[d * steps + c]
            loading_grad_ref[d, :, cols] = dot(fac[d], sensitivity) / path_total
            factor_acc[...] += dot(sensitivity, load_t[cols, :])

        factor_t[...] = factor_acc[...].T
        mine = factor_t[pl.ds(pl.multiple_of(d * factor_count, factor_count), factor_count), :]
        g = d // dates_out
        for o in range(n_path):
            grad_send[g, o, lax.rem(d, dates_out)] = mine[
                :, o * path_local : (o + 1) * path_local
            ]

        for late, stage in enumerate(stages, 1):

            @pl.when(d < late)
            def _(late=late, stage=stage):
                stage(d + dates_own - late)

        @pl.when(lax.rem(d, dates_out) == dates_out - 1)
        def _():
            here = me_path * groups + g == me_trade

            @pl.when(here)
            def _():
                pltpu.make_async_copy(
                    grad_send.at[g, 0], grad_recv.at[me_trade], grad_rsem.at[me_trade]
                ).start()

            @pl.when(jnp.logical_not(here))
            def _():
                grad_copy(g, 0).start()

            for o in range(1, n_path):
                grad_copy(g, o).start()

    if n_path > 1:
        wait_all(fac_recv, fac_ssem)
    for d in range(dates_own):
        wait_all(pair_recv.at[d], pair_ssem.at[d])
        wait_all(cross_recv.at[d], cross_ssem.at[d])
        wait_all(span_half.at[d, pl.ds(1, chips - 1)], half_ssem.at[d])
        wait_all(span_other.at[d], other_ssem.at[d])
    for g in range(groups):

        @pl.when(me_path * groups + g != me_trade)
        def _():
            grad_copy(g, 0).wait_send()

        for o in range(1, n_path):
            grad_copy(g, o).wait_send()

    for b in range(n_trade):
        wait_all(grad_recv.at[b], grad_rsem.at[b])
    sums = grad_recv[0]
    for b in range(1, n_trade):
        sums = sums + grad_recv[b]
    factor_grad_ref[...] = sums


def on_device(
    n_path,
    n_trade,
    factors,
    loadings,
    notional,
    strike,
    date_weight,
    loss_spanning,
    loss_local,
    trade_slot,
    span_list,
):
    dates, factor_count, path_local = factors.shape
    trades = loadings.shape[2]
    spans = loss_spanning.shape[0]
    locals_ = loss_local.shape[0]
    width = spans + locals_
    paths = n_path * path_local
    rows = paths // n_trade
    chips = n_trade // 2
    dates_own = dates // n_path
    dates_out = dates // n_trade
    groups = dates_own // dates_out
    chunk = chunk_of(paths, trades)
    vmem = pl.BlockSpec(memory_space=pltpu.VMEM)
    dma = pltpu.SemaphoreType.DMA
    return pl.pallas_call(
        functools.partial(kernel, n_path, n_trade),
        out_shape=(
            jax.ShapeDtypeStruct((dates_own, factor_count, trades), f32),
            jax.ShapeDtypeStruct((dates_out, factor_count, path_local), f32),
        ),
        in_specs=[
            vmem,
            pl.BlockSpec(memory_space=pl.ANY),
            vmem,
            vmem,
            pl.BlockSpec(memory_space=pltpu.SMEM),
            vmem,
            vmem,
            vmem,
            vmem,
        ],
        out_specs=(vmem, vmem),
        scratch_shapes=[
            pltpu.VMEM((dates_own * (trades // chunk), paths, chunk), bf16),
            pltpu.VMEM((trades, width), bf16),
            pltpu.VMEM((width, trades), bf16),
            pltpu.VMEM((dates_own, factor_count, trades), bf16),
            pltpu.VMEM((dates_own, 4 * factor_count, trades), bf16),
            pltpu.VMEM((trades, dates_own * factor_count), bf16),
            pltpu.VMEM((1, trades), f32),
            pltpu.VMEM((max(n_path - 1, 1), dates_own, factor_count, path_local), bf16),
            pltpu.VMEM((dates_own, factor_count, paths), bf16),
            pltpu.VMEM((dates_own, paths, 4 * factor_count), bf16),
            pltpu.VMEM((paths, width), f32),
            pltpu.VMEM((dates_own, 2, chips, rows, spans), f32),
            pltpu.VMEM((dates_own, chips, rows, spans), f32),
            pltpu.VMEM((dates_own, chips, rows, spans), f32),
            pltpu.VMEM((dates_own, chips - 1, rows, spans), f32),
            pltpu.VMEM((dates_own, paths, locals_), bf16),
            pltpu.VMEM((dates_own, chips, rows, spans), bf16),
            pltpu.VMEM((dates_own, chips, rows, spans), bf16),
            pltpu.VMEM((paths, width), bf16),
            pltpu.VMEM((paths, dates_own * factor_count), f32),
            pltpu.VMEM((dates_own * factor_count, paths), f32),
            pltpu.VMEM((groups, n_path, dates_out, factor_count, path_local), f32),
            pltpu.VMEM((n_trade, dates_out, factor_count, path_local), f32),
            dma,
            dma,
            dma,
            dma((dates_own,)),
            dma((dates_own,)),
            dma((dates_own,)),
            dma((dates_own,)),
            dma((dates_own,)),
            dma((dates_own,)),
            dma((dates_own,)),
            dma((dates_own,)),
            dma((groups, n_path)),
            dma((n_trade,)),
        ],
        compiler_params=pltpu.CompilerParams(
            collective_id=0, has_side_effects=True, vmem_limit_bytes=67043328
        ),
    )(
        factors,
        loadings,
        notional[None],
        strike[None],
        date_weight,
        loss_spanning[None],
        loss_local[None],
        trade_slot[None],
        span_list[None],
    )


def solution(mesh):
    return jax.shard_map(
        functools.partial(on_device, mesh.shape["path"], mesh.shape["trade"]),
        mesh=mesh,
        in_specs=(
            P(None, None, "path"),
            P(None, None, "trade"),
            P("trade"),
            P("trade"),
            P(),
            P(),
            P("trade"),
            P("trade"),
            P("trade"),
        ),
        out_specs=(P("path", None, "trade"), P("trade", None, "path")),
        check_vma=False,
    )
```

```python
import functools
import math

import jax
import jax.numpy as jnp
from jax import lax
from jax.experimental import pallas as pl
from jax.experimental.pallas import tpu as pltpu
from jax.sharding import PartitionSpec as P

smoothing = 0.5
MESH = pl.DeviceIdType.MESH
bf16 = jnp.bfloat16
f32 = jnp.float32


def chunk_of(paths, trades):
    return math.gcd(trades, (1 << 20) // paths)


def dot(a, b):
    return jnp.dot(a, b, preferred_element_type=f32)


def kernel(
    n_path,
    n_trade,
    factors_ref,
    loadings_ref,
    notional_ref,
    strike_ref,
    date_weight_ref,
    loss_span_ref,
    loss_local_ref,
    slot_ref,
    span_ref,
    loading_grad_ref,
    factor_grad_ref,
    growth,
    table,
    table_t,
    load_own,
    load_wide,
    offset,
    fac_recv,
    fac,
    fac_t,
    total,
    part,
    pair_recv,
    chip_sum,
    cross_recv,
    local_w,
    span_half,
    span_other,
    slot_w,
    factor_acc,
    grad_send,
    grad_recv,
    load_sem,
    fac_ssem,
    fac_rsem,
    pair_ssem,
    pair_rsem,
    cross_ssem,
    cross_rsem,
    half_ssem,
    half_rsem,
    other_ssem,
    other_rsem,
    grad_ssem,
    grad_rsem,
):
    me_path = lax.axis_index("path")
    me_trade = lax.axis_index("trade")
    dates, factor_count, path_local = factors_ref.shape
    dates_own = dates // n_path
    dates_out = dates // n_trade
    groups = dates_own // dates_out
    trades = loadings_ref.shape[2]
    spans = loss_span_ref.shape[1]
    span_slots = span_ref.shape[1]
    locals_ = loss_local_ref.shape[1]
    slots = span_slots + locals_
    path_total = n_path * path_local
    chunk = chunk_of(path_total, trades)
    steps = trades // chunk
    first_date = me_path * dates_own
    rows = path_total // n_trade
    chips = n_trade // 2
    me_chip = me_trade // 2
    me_core = lax.rem(me_trade, 2)
    sibling = me_trade + 1 - 2 * me_core

    def path_at(step):
        return lax.rem(me_path + step + n_path, n_path)

    def trade_at(step):
        return lax.rem(me_trade + step + n_trade, n_trade)

    def chip_at(step):
        return lax.rem(me_chip + step + chips, chips)

    def columns(c):
        return pl.ds(pl.multiple_of(c * chunk, chunk), chunk)

    load = pltpu.make_async_copy(
        loadings_ref.at[pl.ds(first_date, dates_own)], load_own, load_sem
    )
    load.start()

    barrier = pltpu.get_barrier_semaphore()
    for a in range(n_path):
        for b in range(n_trade):
            if a or b:
                pl.semaphore_signal(
                    barrier,
                    inc=1,
                    device_id={"path": path_at(a), "trade": trade_at(b)},
                    device_id_type=MESH,
                )
    set_match = (
        lax.broadcasted_iota(jnp.int32, (spans, span_slots), 0) == span_ref[...]
    ).astype(f32).astype(bf16)

    @pl.loop(0, steps)
    def _(c):
        cols = columns(c)
        hot = (
            lax.broadcasted_iota(jnp.int32, (slots, chunk), 0) == slot_ref[:, cols]
        ).astype(f32)
        span_hot = dot(set_match, hot[:span_slots].astype(bf16))
        both = jnp.concatenate([span_hot, hot[span_slots:]], axis=0)
        table_t[:, cols] = both.astype(bf16)
        table[cols, :] = both.T.astype(bf16)

    pl.semaphore_wait(barrier, n_path * n_trade - 1)

    def fac_copy(o):
        there = path_at(o)
        return pltpu.make_async_remote_copy(
            src_ref=factors_ref.at[pl.ds(there * dates_own, dates_own)],
            dst_ref=fac_recv.at[o - 1],
            send_sem=fac_ssem,
            recv_sem=fac_rsem,
            device_id={"path": there},
            device_id_type=MESH,
        )

    for o in range(1, n_path):
        fac_copy(o).start()

    offset[...] = notional_ref[...] * strike_ref[...]
    load.wait()

    for d in range(dates_own):
        row = load_own[d]
        load_wide[d] = jnp.concatenate([row, row, row, row], axis=0)

    if n_path > 1:
        pltpu.make_async_copy(fac_recv, fac_recv, fac_rsem).wait()

    for d in range(dates_own):
        blocks = [factors_ref[first_date + d]]
        blocks += [fac_recv[o - 1, d] for o in range(1, n_path)]
        whole = jnp.concatenate(blocks, axis=1)
        fac[d] = whole
        scaled = whole.astype(f32) * f32(math.log2(math.e))
        high = scaled.astype(bf16).astype(f32)
        middle = (scaled - high).astype(bf16).astype(f32)
        low = scaled - high - middle
        split = jnp.concatenate([high, middle, low, jnp.zeros_like(low)], axis=0)
        fac_t[d] = split.T.astype(bf16)

    def wait_all(buffer, sem):
        pltpu.make_async_copy(buffer, buffer, sem).wait()

    def send_pair(d):
        pltpu.make_async_remote_copy(
            src_ref=part.at[d, 1 - me_core],
            dst_ref=pair_recv.at[d],
            send_sem=pair_ssem.at[d],
            recv_sem=pair_rsem.at[d],
            device_id={"trade": sibling},
            device_id_type=MESH,
        ).start()

    def send_cross(d):
        wait_all(pair_recv.at[d], pair_rsem.at[d])
        chip_sum[d] = part[d, me_core] + pair_recv[d]
        for o in range(1, chips):
            there = chip_at(o)
            pltpu.make_async_remote_copy(
                src_ref=chip_sum.at[d, there],
                dst_ref=cross_recv.at[d, o - 1],
                send_sem=cross_ssem.at[d],
                recv_sem=cross_rsem.at[d],
                device_id={"trade": there * 2 + me_core},
                device_id_type=MESH,
            ).start()

    def send_half(d):
        wait_all(cross_recv.at[d], cross_rsem.at[d])
        sums = chip_sum[d, me_chip]
        for o in range(1, chips):
            sums = sums + cross_recv[d, o - 1]
        weight = date_weight_ref[first_date + d]
        span_half[d, 0] = (
            weight * loss_span_ref[...] * jax.nn.sigmoid(sums / smoothing)
        ).astype(bf16)
        for o in range(1, chips):
            pltpu.make_async_remote_copy(
                src_ref=span_half.at[d, 0],
                dst_ref=span_half.at[d, o],
                send_sem=half_ssem.at[d],
                recv_sem=half_rsem.at[d],
                device_id={"trade": chip_at(o) * 2 + me_core},
                device_id_type=MESH,
            ).start()

    def send_other(d):
        wait_all(span_half.at[d, pl.ds(1, chips - 1)], half_rsem.at[d])
        pltpu.make_async_remote_copy(
            src_ref=span_half.at[d],
            dst_ref=span_other.at[d],
            send_sem=other_ssem.at[d],
            recv_sem=other_rsem.at[d],
            device_id={"trade": sibling},
            device_id_type=MESH,
        ).start()

    lag = max(1, (dates_own - 1) // 3)
    stages = ((lag, send_cross), (2 * lag, send_half), (3 * lag, send_other))

    @pl.loop(0, dates_own)
    def _(d):
        total[...] = jnp.zeros_like(total)

        @pl.loop(0, steps, unroll=True)
        def _(c):
            cols = columns(c)
            exponent = dot(fac_t[d], load_wide[d, :, cols])
            grown = jnp.exp2(exponent) * notional_ref[:, cols]
            growth[d * steps + c] = grown.astype(bf16)
            values = (grown - offset[:, cols]).astype(bf16)
            total[...] += dot(values, table[cols, :])

        for r in range(n_trade):
            part[d, r % 2, r // 2] = total[r * rows : (r + 1) * rows, :spans]
        send_pair(d)
        weight = date_weight_ref[first_date + d]
        local_w[d] = (
            weight * loss_local_ref[...] * jax.nn.sigmoid(total[:, spans:] / smoothing)
        ).astype(bf16)

        for late, stage in stages:

            @pl.when(d >= late)
            def _(late=late, stage=stage):
                stage(d - late)

    def grad_copy(g, o):
        return pltpu.make_async_remote_copy(
            src_ref=grad_send.at[g, o],
            dst_ref=grad_recv.at[me_trade],
            send_sem=grad_ssem.at[g, o],
            recv_sem=grad_rsem.at[me_trade],
            device_id={"path": path_at(-o), "trade": me_path * groups + g},
            device_id_type=MESH,
        )

    @pl.loop(0, dates_own)
    def _(d):
        wait_all(span_other.at[d], other_rsem.at[d])
        for o in range(chips):
            for core, source in ((me_core, span_half), (1 - me_core, span_other)):
                start = pl.multiple_of((chip_at(-o) * 2 + core) * rows, rows)
                slot_w[pl.ds(start, rows), :spans] = source[d, o]
        slot_w[:, spans:] = local_w[d]
        factor_acc[...] = jnp.zeros_like(factor_acc)

        @pl.loop(0, steps, unroll=True)
        def _(c):
            cols = columns(c)
            weight = dot(slot_w[...], table_t[:, cols]).astype(bf16)
            sensitivity = weight * growth[d * steps + c]
            loading_grad_ref[d, :, cols] = dot(fac[d], sensitivity) / path_total
            factor_acc[...] += lax.dot_general(
                load_own[d, :, cols],
                sensitivity,
                (((1,), (1,)), ((), ())),
                preferred_element_type=f32,
            )

        g = d // dates_out
        for o in range(n_path):
            grad_send[g, o, lax.rem(d, dates_out)] = factor_acc[
                :, o * path_local : (o + 1) * path_local
            ]

        for late, stage in stages:

            @pl.when(d < late)
            def _(late=late, stage=stage):
                stage(d + dates_own - late)

        @pl.when(lax.rem(d, dates_out) == dates_out - 1)
        def _():
            here = me_path * groups + g == me_trade

            @pl.when(here)
            def _():
                pltpu.make_async_copy(
                    grad_send.at[g, 0], grad_recv.at[me_trade], grad_rsem.at[me_trade]
                ).start()

            @pl.when(jnp.logical_not(here))
            def _():
                grad_copy(g, 0).start()

            for o in range(1, n_path):
                grad_copy(g, o).start()

    if n_path > 1:
        wait_all(fac_recv, fac_ssem)
    for d in range(dates_own):
        wait_all(pair_recv.at[d], pair_ssem.at[d])
        wait_all(cross_recv.at[d], cross_ssem.at[d])
        wait_all(span_half.at[d, pl.ds(1, chips - 1)], half_ssem.at[d])
        wait_all(span_other.at[d], other_ssem.at[d])
    for g in range(groups):

        @pl.when(me_path * groups + g != me_trade)
        def _():
            grad_copy(g, 0).wait_send()

        for o in range(1, n_path):
            grad_copy(g, o).wait_send()

    for b in range(n_trade):
        wait_all(grad_recv.at[b], grad_rsem.at[b])
    sums = grad_recv[0]
    for b in range(1, n_trade):
        sums = sums + grad_recv[b]
    factor_grad_ref[...] = sums


def on_device(
    n_path,
    n_trade,
    factors,
    loadings,
    notional,
    strike,
    date_weight,
    loss_spanning,
    loss_local,
    trade_slot,
    span_list,
):
    dates, factor_count, path_local = factors.shape
    trades = loadings.shape[2]
    spans = loss_spanning.shape[0]
    locals_ = loss_local.shape[0]
    width = spans + locals_
    paths = n_path * path_local
    rows = paths // n_trade
    chips = n_trade // 2
    dates_own = dates // n_path
    dates_out = dates // n_trade
    groups = dates_own // dates_out
    chunk = chunk_of(paths, trades)
    vmem = pl.BlockSpec(memory_space=pltpu.VMEM)
    dma = pltpu.SemaphoreType.DMA
    return pl.pallas_call(
        functools.partial(kernel, n_path, n_trade),
        out_shape=(
            pltpu.VMEM((dates_own, factor_count, trades), f32),
            pltpu.VMEM((dates_out, factor_count, path_local), f32),
        ),
        in_specs=[
            vmem,
            pl.BlockSpec(memory_space=pl.ANY),
            vmem,
            vmem,
            pl.BlockSpec(memory_space=pltpu.SMEM),
            vmem,
            vmem,
            vmem,
            vmem,
        ],
        out_specs=(vmem, vmem),
        scratch_shapes=[
            pltpu.VMEM((dates_own * (trades // chunk), paths, chunk), bf16),
            pltpu.VMEM((trades, width), bf16),
            pltpu.VMEM((width, trades), bf16),
            pltpu.VMEM((dates_own, factor_count, trades), bf16),
            pltpu.VMEM((dates_own, 4 * factor_count, trades), bf16),
            pltpu.VMEM((1, trades), f32),
            pltpu.VMEM((max(n_path - 1, 1), dates_own, factor_count, path_local), bf16),
            pltpu.VMEM((dates_own, factor_count, paths), bf16),
            pltpu.VMEM((dates_own, paths, 4 * factor_count), bf16),
            pltpu.VMEM((paths, width), f32),
            pltpu.VMEM((dates_own, 2, chips, rows, spans), f32),
            pltpu.VMEM((dates_own, chips, rows, spans), f32),
            pltpu.VMEM((dates_own, chips, rows, spans), f32),
            pltpu.VMEM((dates_own, chips - 1, rows, spans), f32),
            pltpu.VMEM((dates_own, paths, locals_), bf16),
            pltpu.VMEM((dates_own, chips, rows, spans), bf16),
            pltpu.VMEM((dates_own, chips, rows, spans), bf16),
            pltpu.VMEM((paths, width), bf16),
            pltpu.VMEM((factor_count, paths), f32),
            pltpu.VMEM((groups, n_path, dates_out, factor_count, path_local), f32),
            pltpu.VMEM((n_trade, dates_out, factor_count, path_local), f32),
            dma,
            dma,
            dma,
            dma((dates_own,)),
            dma((dates_own,)),
            dma((dates_own,)),
            dma((dates_own,)),
            dma((dates_own,)),
            dma((dates_own,)),
            dma((dates_own,)),
            dma((dates_own,)),
            dma((groups, n_path)),
            dma((n_trade,)),
        ],
        compiler_params=pltpu.CompilerParams(
            collective_id=0, has_side_effects=True, vmem_limit_bytes=61 << 20
        ),
    )(
        factors,
        loadings,
        notional[None],
        strike[None],
        date_weight,
        loss_spanning[None],
        loss_local[None],
        trade_slot[None],
        span_list[None],
    )


def solution(mesh):
    return jax.shard_map(
        functools.partial(on_device, mesh.shape["path"], mesh.shape["trade"]),
        mesh=mesh,
        in_specs=(
            P(None, None, "path"),
            P(None, None, "trade"),
            P("trade"),
            P("trade"),
            P(),
            P(),
            P("trade"),
            P("trade"),
            P("trade"),
        ),
        out_specs=(P("path", None, "trade"), P("trade", None, "path")),
        check_vma=False,
    )
```
